256 devices in a mesh: rep: 64 (over x_lo, z, y), blk: 4 (over x_hi, core).
Axes of the slice: x: 4 (x_hi: 2, x_lo: 2; x = x_hi * 2 + x_lo), y: 4, z: 8, core: 2. Of those that a mesh axis runs over, the one named last changes fastest.
Arguments:
- encoded: bfloat16 [1024, 512, 512], P(('rep', 'blk')), may hold values from -6 to 6
- queries: bfloat16 [1024, 512], P('blk'), may hold values from -0.25 to 0.25
- classifiers: bfloat16 [1024, 512], P('blk'), may hold values from -1 to 1
- lengths: int32 [1024], P(('rep', 'blk')), may hold values from 1 to 512, 393216 in all
- beam: int32 [1024, 1024], P(('rep', 'blk')), may hold values 0 or 1
- logit_grad: float32 [1024, 1024], P(('rep', 'blk')), may hold values from -24 to 24
Outputs:
- logits: float32 [1024, 1024], P(('rep', 'blk'))
- encoded_grad: bfloat16 [1024, 512, 512], P(('rep', 'blk'))
- label_grad: float32 [1024, 1024], P('blk')
The draws below stay inside these ranges and needn't reach their ends.
Inputs may be any that keep to these rules, and one draw needn't show every extreme that they name: `lengths`: every document has at least one real token, and some document has exactly 512.
All inputs are finite; a program needn't handle non-finite values. No bound on the sum of `lengths` or of `beam` on one device may be relied on, other than what follows from the above.
Results may differ from the reference program's by a relative error of at most 0.0058.
Values may be sent and summed in bfloat16 or wider, within the bound.
A program may use at most 64 MiB of HBM per device.

```python
import math
import jax
import jax.numpy as jnp
import numpy as np
from jax import lax

E = 512
LABELS = 1024
L = 512
DOCS = 1024


def touch_ends(entries, stream_key, low, top_value):
    index_at = [jax.random.randint(jax.random.fold_in(stream_key, axis), (), 0, length) for axis, length in enumerate(entries.shape)]
    main_axis = entries.shape.index(max(entries.shape))
    next_to = index_at[:main_axis] + [(index_at[main_axis] + 1) % entries.shape[main_axis]] + index_at[main_axis + 1:]
    return entries.at[tuple(index_at)].set(low).at[tuple(next_to)].set(top_value)


def strengthened(result, rng, source, target, parts, factor):
    owner, partner = [(jnp.arange(result.shape[dim]) // (result.shape[dim] // parts)).reshape([-1 if axis == dim else 1 for axis in range(result.ndim)]) for dim in (source, target)]
    chosen = jax.random.permutation(rng, parts)[partner]
    strong = (owner == chosen) | (owner == (partner + parts // 2) % parts)
    return jnp.where(strong, factor * result, result)


def steps_of(key, extent, split, least, high):
    def one(axis_at, shards_of):
        draws = jax.random.uniform(jax.random.fold_in(jax.random.fold_in(key, 6), axis_at), (shards_of,), jnp.float32, least / len(split), high / len(split))
        return jnp.repeat(jnp.exp(draws), extent[axis_at] // shards_of).reshape((-1,) + (1,) * (len(extent) - axis_at - 1))

    level = one(*split[0])
    for cut in split[1:]:
        level = level * one(*cut)
    return level


def split_up(count, total, most, skew):
    weights = [(1 << 20) // math.isqrt(standing ** skew) + 1 for standing in range(2, count + 1)]
    surplus, counts = total - most - (count - 1), [1] * (count - 1)
    while surplus > 0:
        movable = [i for i in range(count - 1) if counts[i] < most]
        pool, budget = sum([weights[i] for i in movable]), surplus
        for i in movable:
            more = min(most - counts[i], max(1, budget * weights[i] // pool), surplus)
            counts[i] = counts[i] + more
            surplus = surplus - more
    return np.array([most] + counts)


def ragged_sizes(own_key, count, total, bound, slope):
    if count == 2:
        one = jax.random.randint(own_key, (), max(1, total - bound), min(bound, total - 1) + 1)
        return jnp.stack([one, total - one])
    sizes = jnp.asarray(split_up(count, total, bound, slope), jnp.int32)
    pairs = (count - 1) // 2
    source_of, receiver = sizes[1:1 + 2 * pairs:2], sizes[2:2 + 2 * pairs:2]
    room = jnp.minimum(source_of - 1, bound - receiver)
    moved = jax.random.randint(jax.random.fold_in(own_key, 1), (pairs,), 0, 1 << 20) % (room + 1)
    sizes = sizes.at[1:1 + 2 * pairs:2].set(source_of - moved).at[2:2 + 2 * pairs:2].set(receiver + moved)
    return sizes[jax.random.permutation(jax.random.fold_in(own_key, 2), count)]


def centred(own_key, shape, scale, limit, split=(), dtype=jnp.bfloat16):
    loudness = steps_of(own_key, shape, split, -0.22, 0.18) if split else 1.0
    array = jax.random.normal(own_key, shape, jnp.float32) * scale * loudness
    return jnp.minimum(jnp.maximum(array, -limit), limit).astype(dtype)


def heavy_noise(own_key, dims, deviation, most, cuts, heavy, dtype=jnp.bfloat16):
    entries = deviation * jax.random.normal(own_key, dims, jnp.float32)
    if cuts:
        entries = entries * steps_of(own_key, dims, cuts, -0.22, 0.18)
    return jnp.clip(strengthened(entries, jax.random.fold_in(own_key, 3), *heavy), -most, most).astype(dtype)


def setup_inputs(seed: int = 0) -> dict:
    splits = jax.random.split(jax.random.key(seed), 7)
    return {
        "encoded": centred(splits[0], (DOCS, L, E), 1.0, 6.0, ((0, 256),)),
        "queries": centred(splits[1], (LABELS, E), E ** -0.5, 0.25, ((0, 4),)),
        "classifiers": centred(splits[2], (LABELS, E), (E // 16) ** -0.5, 1.0, ((0, 4),)),
        "lengths": ragged_sizes(splits[3], DOCS, DOCS * L * 3 // 4, L, 1).astype(jnp.int32),
        "beam": touch_ends((jax.random.randint(splits[4], (DOCS, LABELS), 0, 4) < 1).astype(jnp.int32), jax.random.fold_in(splits[4], 1), 0, 1),
        "logit_grad": heavy_noise(splits[5], (DOCS, LABELS), 1.0, 24.0, ((0, 256),), (0, 1, 256, 6.0), jnp.float32),
    }


def one_document(states, length, beam_row, grad_row, queries, classifiers):
    scores = jnp.dot(queries, states.T, preferred_element_type=jnp.float32)
    valid = jnp.arange(states.shape[0]) < length
    expo = jnp.where(valid[None, :], jnp.exp(scores), 0.0)
    attn = expo / jnp.sum(expo, axis=1, keepdims=True)
    attn_b = attn.astype(jnp.bfloat16)
    context = jnp.dot(attn_b, states, preferred_element_type=jnp.float32)
    cls_f = classifiers.astype(jnp.float32)
    logit = jnp.sum(context * cls_f, axis=1)
    g_row = grad_row * beam_row.astype(jnp.float32)
    ctx_grad = (g_row[:, None] * cls_f).astype(jnp.bfloat16)
    attn_grad = jnp.dot(ctx_grad, states.T, preferred_element_type=jnp.float32)
    score_grad = (attn * (attn_grad - jnp.sum(attn * attn_grad, axis=1, keepdims=True))).astype(jnp.bfloat16)
    query_grad = jnp.dot(score_grad, states, preferred_element_type=jnp.float32)
    class_grad = g_row[:, None] * context
    state_grad = jnp.dot(attn_b.T, ctx_grad, preferred_element_type=jnp.float32) + jnp.dot(score_grad.T, queries, preferred_element_type=jnp.float32)
    return logit, query_grad, class_grad, state_grad.astype(jnp.bfloat16)


def reference(encoded, queries, classifiers, lengths, beam, logit_grad):
    def step(carry, items):
        states, length, beam_row, grad_row = items
        logit, query_grad, class_grad, state_grad = one_document(states, length, beam_row, grad_row, queries, classifiers)
        return (carry[0] + query_grad, carry[1] + class_grad), (logit, state_grad)

    zeros = jnp.zeros((LABELS, E), jnp.float32)
    sums, outs = lax.scan(step, (zeros, zeros), (encoded, lengths, beam, logit_grad))
    label_grad = jnp.concatenate([sums[0], sums[1]], axis=1)
    return outs[0], outs[1], label_grad
```

```python
import jax
import jax.numpy as jnp
from jax import lax
from jax.experimental import pallas as pl
from jax.experimental.pallas import tpu as pltpu
from jax.sharding import PartitionSpec as P

MESH = pl.DeviceIdType.MESH
F32 = jnp.float32
BF16 = jnp.bfloat16
E = 512
L = 512
DOCS = 4
T = DOCS * L
HB = 128
NEG = -1e30


def body(
    enc_hbm, q_hbm, c_hbm, len_ref, beam_ref, grad_ref,
    logit_ref, eg_ref, lg_ref,
    S, ST, W, GA, SP, G, acc, eacc,
    dsend, drecv, ysend, yrecv, yown, xsend, xrecv, xown, zsend, zrecv, zown, agp,
    lsem, gs, gr, ds, dr, ys, yr, xs, xr, zs, zr, as_, ar, ps, pr,
):
    rep = lax.axis_index("rep")
    blk = lax.axis_index("blk")
    x_lo = rep // 32
    z = (rep // 4) % 8
    y = rep % 4
    x_hi = blk // 2
    core = blk % 2

    def dev(xl, zz, yy, xh, cc):
        return ((xl * 8 + zz) * 4 + yy, xh * 2 + cc)

    partner = dev(x_lo, z, y, x_hi, 1 - core)
    across = dev(1 - x_lo, z, y, 1 - x_hi, core)
    across2 = dev(x_lo, z, y, 1 - x_hi, core)
    xpair = dev(1 - x_lo, z, y, x_hi, core)
    place = y * 2 + x_lo

    def ynb(k):
        return dev(x_lo, z, (y + k) % 4, x_hi, core)

    def znb(k):
        return dev(x_lo, (z + k) % 8, y, x_hi, core)

    def pnb(k):
        pp = (place + k) % 8
        return dev(pp % 2, z, pp // 2, x_hi, core)

    def local(src, dst, i):
        cp = pltpu.make_async_copy(src, dst, lsem.at[i])
        cp.start()
        return cp

    def remote(src, dst, ssem, rsem, to):
        return pltpu.make_async_remote_copy(
            src_ref=src, dst_ref=dst, send_sem=ssem, recv_sem=rsem,
            device_id=to, device_id_type=MESH,
        )

    pending = []

    def go(cp):
        cp.start()
        pending.append(cp)
        return cp

    weights = []
    for p in range(2):
        weights.append(local(q_hbm.at[pl.ds(p * HB, HB)], W.at[p, pl.ds(0, HB)], 2 * p))
        weights.append(local(c_hbm.at[pl.ds(p * HB, HB)], W.at[p, pl.ds(HB, HB)], 2 * p + 1))
    states = [local(enc_hbm.at[pl.ds(d * L, L)], S.at[pl.ds(d * L, L)], 4 + d) for d in range(DOCS)]

    barrier = pltpu.get_barrier_semaphore()
    greet = [partner, across, across2] + [znb(k) for k in range(1, 8)] + [pnb(k) for k in range(1, 8)]
    for to in greet:
        pl.semaphore_signal(barrier, inc=1, device_id=to, device_id_type=MESH)
    G[...] = grad_ref[...] * beam_ref[...].astype(F32)
    for cp in weights:
        cp.wait()
    pl.semaphore_wait(barrier, len(greet))

    to_partner = [go(remote(W.at[p], W.at[2 + p], gs.at[p], gr.at[p], partner)) for p in range(2)]
    to_across = [go(remote(W.at[p], W.at[5 + 2 * p], gs.at[2 + p], gr.at[2 + p], across)) for p in range(2)]
    to_fwd = [remote(W.at[5 + 2 * p], W.at[4 + 2 * p], gs.at[4 + p], gr.at[4 + p], partner) for p in range(2)]

    for d in range(DOCS):
        states[d].wait()
        ST[:, pl.ds(d * L, L)] = S[pl.ds(d * L, L), :].T

    own0 = blk * 256
    par0 = (x_hi * 2 + 1 - core) * 256
    far_own0 = ((1 - x_hi) * 2 + core) * 256
    far_par0 = ((1 - x_hi) * 2 + 1 - core) * 256
    starts = [own0, own0 + HB, par0, par0 + HB, far_par0, far_own0, far_par0 + HB, far_own0 + HB]

    row = lax.broadcasted_iota(jnp.int32, (L, HB), 0)

    def slot(k):
        at = pl.ds(pl.multiple_of(starts[k], HB), HB)
        w = W[k]
        for d in range(DOCS):
            SP[pl.ds(d * L, L), :] = lax.dot_general(
                S[pl.ds(d * L, L), :], w, (((1,), (1,)), ((), ())), preferred_element_type=F32
            )
        for d in range(DOCS):
            rows = pl.ds(d * L, L)
            sc = jnp.where(row < len_ref[d], SP[rows, pl.ds(0, HB)], NEG)
            pr_ = SP[rows, pl.ds(HB, HB)]
            ex = jnp.exp(sc - jnp.max(sc, axis=0, keepdims=True))
            inv = 1.0 / jnp.sum(ex, axis=0, keepdims=True)
            lg = jnp.sum(ex * pr_, axis=0, keepdims=True) * inv
            logit_ref[pl.ds(d, 1), at] = lg
            ag = ex * (inv * G[pl.ds(d, 1), at])
            GA[rows, pl.ds(k * 256 + HB, HB)] = ag.astype(BF16)
            GA[rows, pl.ds(k * 256, HB)] = (ag * (pr_ - lg)).astype(BF16)
        return jnp.dot(ST[...], GA[:, pl.ds(k * 256, 256)], preferred_element_type=F32)

    def state_grad(first):
        def tile(i, carry):
            rows = pl.ds(pl.multiple_of(i * 256, 256), 256)
            if first:
                eacc[rows, :] = jnp.dot(
                    GA[rows, pl.ds(0, 1024)], W[pl.ds(0, 4)].reshape(1024, E), preferred_element_type=F32
                )
            else:
                eg_ref[rows, :] = (
                    eacc[rows, :]
                    + jnp.dot(
                        GA[rows, pl.ds(1024, 1024)], W[pl.ds(4, 4)].reshape(1024, E), preferred_element_type=F32
                    )
                ).astype(BF16)
            return carry

        return tile

    def die_send(j, value):
        dsend[j] = value.astype(BF16)
        return go(remote(dsend.at[j], drecv.at[j], ds.at[j], dr.at[j], partner))

    def y_send(j, dcp, own):
        dcp.wait_recv()
        total = own + drecv[j].astype(F32)
        yown[j] = total.reshape(4, 128, 256)
        ysend[j] = total.astype(BF16).reshape(4, 128, 256)
        return [
            go(remote(ysend.at[j, (y + k) % 4], yrecv.at[j, k - 1], ys.at[j, k - 1], yr.at[j, k - 1], ynb(k)))
            for k in range(1, 4)
        ]

    def y_sum(j, cps):
        for cp in cps:
            cp.wait_recv()
        total = yown[j, y]
        for k in range(3):
            total = total + yrecv[j, k].astype(F32)
        return total

    def x_send_home(p, cps):
        total = y_sum(p, cps).reshape(2, 64, 256)
        xown[p] = total
        xsend[p] = total.astype(BF16)
        return go(remote(xsend.at[p, 1 - x_lo], xrecv.at[p, 0], xs.at[p, 0], xr.at[p, 0], xpair))

    def x_send_away(p, cps):
        total = y_sum(2 + p, cps).reshape(2, 64, 256)
        xsend[2 + p] = total.astype(BF16)
        return [
            go(remote(xsend.at[2 + p, x_lo], xrecv.at[p, 1], xs.at[p, 1], xr.at[p, 1], across2)),
            go(remote(xsend.at[2 + p, 1 - x_lo], xrecv.at[p, 2], xs.at[p, 2], xr.at[p, 2], across)),
        ]

    def z_send(p, cps):
        for cp in cps:
            cp.wait_recv()
        total = xown[p, x_lo]
        for k in range(3):
            total = total + xrecv[p, k].astype(F32)
        for i in range(4):
            for j in range(2):
                piece = total[i * 16 : (i + 1) * 16, j * 128 : (j + 1) * 128]
                zown[p, i * 2 + j] = piece
                zsend[p, i * 2 + j] = piece.astype(BF16)
        return [
            go(remote(zsend.at[p, (z + k) % 8], zrecv.at[p, k - 1], zs.at[p, k - 1], zr.at[p, k - 1], znb(k)))
            for k in range(1, 8)
        ]

    def az_send(p, cps):
        for cp in cps:
            cp.wait_recv()
        total = zown[p, z]
        for k in range(7):
            total = total + zrecv[p, k].astype(F32)
        agp[p, place, z] = total.astype(BF16)
        return [
            go(remote(agp.at[p, place, z], agp.at[p, place, z], as_.at[p, k - 1], ar.at[p, k - 1], znb(k)))
            for k in range(1, 8)
        ]

    def ap_send(p, cps):
        for cp in cps:
            cp.wait_recv()
        return [
            go(remote(agp.at[p, place], agp.at[p, place], ps.at[p, k - 1], pr.at[p, k - 1], pnb(k)))
            for k in range(1, 8)
        ]

    def finish(p, cps):
        for cp in cps:
            cp.wait_recv()
        for j in range(2):
            parts = [agp[p, a, i * 2 + j] for a in range(8) for i in range(4)]
            whole = jnp.concatenate(parts, axis=0).astype(F32)
            lg_ref[pl.ds(p * HB, HB), pl.ds(j * E, E)] = whole.T

    acc[0] = slot(0)
    acc[1] = slot(1)
    to_partner[0].wait_recv()
    d0 = die_send(0, slot(2))
    to_partner[1].wait_recv()
    d1 = die_send(1, slot(3))
    y0 = y_send(0, d0, acc[0])
    to_across[0].wait_recv()
    go(to_fwd[0])
    y1 = y_send(1, d1, acc[1])
    lax.fori_loop(0, 8, state_grad(True), 0)
    xa0 = x_send_home(0, y0)
    xa1 = x_send_home(1, y1)
    to_fwd[0].wait_recv()
    d2 = die_send(2, slot(4))
    y2 = y_send(2, d2, slot(5))
    to_across[1].wait_recv()
    go(to_fwd[1])
    to_fwd[1].wait_recv()
    d3 = die_send(3, slot(6))
    xb0 = x_send_away(0, y2)
    y3 = y_send(3, d3, slot(7))
    z0 = z_send(0, [xa0] + xb0)
    lax.fori_loop(0, 3, state_grad(False), 0)
    xb1 = x_send_away(1, y3)
    lax.fori_loop(3, 5, state_grad(False), 0)
    az0 = az_send(0, z0)
    z1 = z_send(1, [xa1] + xb1)
    lax.fori_loop(5, 8, state_grad(False), 0)
    ap0 = ap_send(0, az0)
    az1 = az_send(1, z1)
    ap1 = ap_send(1, az1)
    finish(0, ap0)
    finish(1, ap1)
    for cp in pending:
        cp.wait_send()


def per_device(encoded, queries, classifiers, lengths, beam, logit_grad):
    any_spec = pl.BlockSpec(memory_space=pl.ANY)
    vm = pl.BlockSpec(memory_space=pltpu.VMEM)
    dma = pltpu.SemaphoreType.DMA
    logits, eg, lg = pl.pallas_call(
        body,
        out_shape=(
            jax.ShapeDtypeStruct((DOCS, 1024), F32),
            jax.ShapeDtypeStruct((T, E), BF16),
            jax.ShapeDtypeStruct((256, 1024), F32),
        ),
        in_specs=[any_spec, any_spec, any_spec, pl.BlockSpec(memory_space=pltpu.SMEM), vm, vm],
        out_specs=(vm, vm, vm),
        scratch_shapes=[
            pltpu.VMEM((T, E), BF16),
            pltpu.VMEM((E, T), BF16),
            pltpu.VMEM((8, 256, E), BF16),
            pltpu.VMEM((T, 2048), BF16),
            pltpu.VMEM((T, 256), F32),
            pltpu.VMEM((DOCS, 1024), F32),
            pltpu.VMEM((2, E, 256), F32),
            pltpu.VMEM((T, E), F32),
            pltpu.VMEM((4, E, 256), BF16),
            pltpu.VMEM((4, E, 256), BF16),
            pltpu.VMEM((4, 4, 128, 256), BF16),
            pltpu.VMEM((4, 3, 128, 256), BF16),
            pltpu.VMEM((4, 4, 128, 256), F32),
            pltpu.VMEM((4, 2, 64, 256), BF16),
            pltpu.VMEM((2, 3, 64, 256), BF16),
            pltpu.VMEM((2, 2, 64, 256), F32),
            pltpu.VMEM((2, 8, 16, 128), BF16),
            pltpu.VMEM((2, 7, 16, 128), BF16),
            pltpu.VMEM((2, 8, 16, 128), F32),
            pltpu.VMEM((2, 8, 8, 16, 128), BF16),
            dma((8,)),
            dma((6,)), dma((6,)),
            dma((4,)), dma((4,)),
            dma((4, 3)), dma((4, 3)),
            dma((2, 3)), dma((2, 3)),
            dma((2, 7)), dma((2, 7)),
            dma((2, 7)), dma((2, 7)),
            dma((2, 7)), dma((2, 7)),
        ],
        compiler_params=pltpu.CompilerParams(
            collective_id=0, has_side_effects=True, vmem_limit_bytes=60 * 1024 * 1024
        ),
        name="attn",
    )(encoded.reshape(T, E), queries, classifiers, lengths, beam, logit_grad)
    return logits, eg.reshape(DOCS, L, E), lg


def solution(mesh):
    in_specs = (
        P(("rep", "blk"), None, None),
        P("blk", None),
        P("blk", None),
        P(("rep", "blk")),
        P(("rep", "blk"), None),
        P(("rep", "blk"), None),
    )
    out_specs = (P(("rep", "blk"), None), P(("rep", "blk"), None, None), P("blk", None))
    return jax.shard_map(
        per_device, mesh=mesh, in_specs=in_specs, out_specs=out_specs, check_vma=False
    )
```

```python
import jax
import jax.numpy as jnp
from jax import lax
from jax.experimental import pallas as pl
from jax.experimental.pallas import tpu as pltpu
from jax.sharding import PartitionSpec as P

MESH = pl.DeviceIdType.MESH
F32 = jnp.float32
BF16 = jnp.bfloat16
E = 512
L = 512
DOCS = 4
T = DOCS * L
HB = 128
NEG = -1e30


def body(
    enc_hbm, q_hbm, c_hbm, len_hbm, beam_hbm, grad_hbm,
    logit_ref, eg_ref, lg_ref,
    S, ST, W, GA, SP, len_ref, beam_ref, grad_ref, G, acc, eacc,
    dsend, drecv, ysend, yrecv, yown, xsend, xrecv, xown, zsend, zrecv, zown, agp,
    lsem, gs, gr, ds, dr, ys, yr, xs, xr, zs, zr, as_, ar, ps, pr,
):
    rep = lax.axis_index("rep")
    blk = lax.axis_index("blk")
    x_lo = rep // 32
    z = (rep // 4) % 8
    y = rep % 4
    x_hi = blk // 2
    core = blk % 2

    def dev(xl, zz, yy, xh, cc):
        return ((xl * 8 + zz) * 4 + yy, xh * 2 + cc)

    partner = dev(x_lo, z, y, x_hi, 1 - core)
    across = dev(1 - x_lo, z, y, 1 - x_hi, core)
    across2 = dev(x_lo, z, y, 1 - x_hi, core)
    xpair = dev(1 - x_lo, z, y, x_hi, core)
    place = y * 2 + x_lo

    def ynb(k):
        return dev(x_lo, z, (y + k) % 4, x_hi, core)

    def znb(k):
        return dev(x_lo, (z + k) % 8, y, x_hi, core)

    def pnb(k):
        pp = (place + k) % 8
        return dev(pp % 2, z, pp // 2, x_hi, core)

    def local(src, dst, i):
        cp = pltpu.make_async_copy(src, dst, lsem.at[i])
        cp.start()
        return cp

    def remote(src, dst, ssem, rsem, to):
        return pltpu.make_async_remote_copy(
            src_ref=src, dst_ref=dst, send_sem=ssem, recv_sem=rsem,
            device_id=to, device_id_type=MESH,
        )

    pending = []

    def go(cp):
        cp.start()
        pending.append(cp)
        return cp

    weights = []
    for p in range(2):
        weights.append(local(q_hbm.at[pl.ds(p * HB, HB)], W.at[p, pl.ds(0, HB)], 2 * p))
        weights.append(local(c_hbm.at[pl.ds(p * HB, HB)], W.at[p, pl.ds(HB, HB)], 2 * p + 1))
    states = [local(enc_hbm.at[pl.ds(d * L, L)], S.at[pl.ds(d * L, L)], 4 + d) for d in range(DOCS)]

    small = [local(beam_hbm, beam_ref, 8), local(grad_hbm, grad_ref, 9), local(len_hbm, len_ref, 10)]

    barrier = pltpu.get_barrier_semaphore()
    greet = [partner, across, across2] + [znb(k) for k in range(1, 8)] + [pnb(k) for k in range(1, 8)]
    for to in greet:
        pl.semaphore_signal(barrier, inc=1, device_id=to, device_id_type=MESH)
    for cp in weights:
        cp.wait()
    pl.semaphore_wait(barrier, len(greet))

    to_partner = [go(remote(W.at[p], W.at[2 + p], gs.at[p], gr.at[p], partner)) for p in range(2)]
    quarter = pl.ds(pl.multiple_of(y * 64, 64), 64)
    to_across1 = go(remote(W.at[1, quarter], W.at[7, quarter], gs.at[2], gr.at[2], across))
    to_across0 = go(remote(W.at[0], W.at[5], gs.at[3], gr.at[3], across))
    to_ring = [
        remote(W.at[7, quarter], W.at[7, quarter], gs.at[5 + k], gr.at[5 + k], ynb(k)) for k in range(1, 4)
    ]
    to_fwd = [remote(W.at[5 + 2 * p], W.at[4 + 2 * p], gs.at[4 + p], gr.at[4 + p], partner) for p in range(2)]

    for cp in small:
        cp.wait()
    G[...] = grad_ref[...] * beam_ref[...].astype(F32)
    for d in range(DOCS):
        states[d].wait()
        ST[:, pl.ds(d * L, L)] = S[pl.ds(d * L, L), :].T

    own0 = blk * 256
    par0 = (x_hi * 2 + 1 - core) * 256
    far_own0 = ((1 - x_hi) * 2 + core) * 256
    far_par0 = ((1 - x_hi) * 2 + 1 - core) * 256
    starts = [own0, own0 + HB, par0, par0 + HB, far_par0, far_own0, far_par0 + HB, far_own0 + HB]

    row = lax.broadcasted_iota(jnp.int32, (L, HB), 0)

    def pair(k):
        ats = [pl.ds(pl.multiple_of(starts[k + i], HB), HB) for i in range(2)]
        w = W[pl.ds(k, 2)].reshape(512, E)
        g = [[G[pl.ds(d, 1), at] for at in ats] for d in range(DOCS)]

        def scores(d):
            SP[pl.ds(d * L, L), :] = lax.dot_general(
                S[pl.ds(d * L, L), :], w, (((1,), (1,)), ((), ())), preferred_element_type=F32
            )

        def soft(d):
            rows = pl.ds(d * L, L)
            valid = row < len_ref[d]
            for i in range(2):
                sc = jnp.where(valid, SP[rows, pl.ds(i * 256, HB)], NEG)
                pr_ = SP[rows, pl.ds(i * 256 + HB, HB)]
                ex = jnp.exp(sc - jnp.max(sc, axis=0, keepdims=True))
                inv = 1.0 / jnp.sum(ex, axis=0, keepdims=True)
                lg = jnp.sum(ex * pr_, axis=0, keepdims=True) * inv
                logit_ref[pl.ds(d, 1), ats[i]] = lg
                ag = ex * (inv * g[d][i])
                GA[rows, pl.ds((k + i) * 256 + HB, HB)] = ag.astype(BF16)
                GA[rows, pl.ds((k + i) * 256, HB)] = (ag * (pr_ - lg)).astype(BF16)

        def lab(d):
            rows = pl.ds(d * L, 2 * L)
            return jnp.dot(ST[:, rows], GA[rows, pl.ds(k * 256, 512)], preferred_element_type=F32)

        scores(0)
        scores(1)
        soft(0)
        scores(2)
        soft(1)
        out = lab(0)
        scores(3)
        soft(2)
        soft(3)
        return out + lab(2)

    def state_grad(first):
        def tile(i, carry):
            rows = pl.ds(pl.multiple_of(i * 256, 256), 256)
            if first:
                eacc[rows, :] = jnp.dot(
                    GA[rows, pl.ds(0, 1024)], W[pl.ds(0, 4)].reshape(1024, E), preferred_element_type=F32
                )
            else:
                eg_ref[rows, :] = (
                    eacc[rows, :]
                    + jnp.dot(
                        GA[rows, pl.ds(1024, 1024)], W[pl.ds(4, 4)].reshape(1024, E), preferred_element_type=F32
                    )
                ).astype(BF16)
            return carry

        return tile

    def die_send(j, value):
        dsend[j] = value.astype(BF16)
        return go(remote(dsend.at[j], drecv.at[j], ds.at[j], dr.at[j], partner))

    def y_send(j, dcp, own):
        dcp.wait_recv()
        total = own + drecv[j].astype(F32)
        yown[j] = total.reshape(4, 128, 256)
        ysend[j] = total.astype(BF16).reshape(4, 128, 256)
        return [
            go(remote(ysend.at[j, (y + k) % 4], yrecv.at[j, k - 1], ys.at[j, k - 1], yr.at[j, k - 1], ynb(k)))
            for k in range(1, 4)
        ]

    def y_sum(j, cps):
        for cp in cps:
            cp.wait_recv()
        total = yown[j, y]
        for k in range(3):
            total = total + yrecv[j, k].astype(F32)
        return total

    def x_send_home(p, cps):
        total = y_sum(p, cps).reshape(2, 64, 256)
        xown[p] = total
        xsend[p] = total.astype(BF16)
        return go(remote(xsend.at[p, 1 - x_lo], xrecv.at[p, 0], xs.at[p, 0], xr.at[p, 0], xpair))

    def x_send_away(p, cps):
        total = y_sum(2 + p, cps).reshape(2, 64, 256)
        xsend[2 + p] = total.astype(BF16)
        return [
            go(remote(xsend.at[2 + p, x_lo], xrecv.at[p, 1], xs.at[p, 1], xr.at[p, 1], across2)),
            go(remote(xsend.at[2 + p, 1 - x_lo], xrecv.at[p, 2], xs.at[p, 2], xr.at[p, 2], across)),
        ]

    def z_send(p, cps):
        for cp in cps:
            cp.wait_recv()
        total = xown[p, x_lo]
        for k in range(3):
            total = total + xrecv[p, k].astype(F32)
        for i in range(4):
            for j in range(2):
                piece = total[i * 16 : (i + 1) * 16, j * 128 : (j + 1) * 128]
                zown[p, i * 2 + j] = piece
                zsend[p, i * 2 + j] = piece.astype(BF16)
        return [
            go(remote(zsend.at[p, (z + k) % 8], zrecv.at[p, k - 1], zs.at[p, k - 1], zr.at[p, k - 1], znb(k)))
            for k in range(1, 8)
        ]

    def az_send(p, cps):
        for cp in cps:
            cp.wait_recv()
        total = zown[p, z]
        for k in range(7):
            total = total + zrecv[p, k].astype(F32)
        agp[p, place, z] = total.astype(BF16)
        return [
            go(remote(agp.at[p, place, z], agp.at[p, place, z], as_.at[p, k - 1], ar.at[p, k - 1], znb(k)))
            for k in range(1, 8)
        ]

    def ap_send(p, cps):
        for cp in cps:
            cp.wait_recv()
        return [
            go(remote(agp.at[p, place], agp.at[p, place], ps.at[p, k - 1], pr.at[p, k - 1], pnb(k)))
            for k in range(1, 8)
        ]

    def finish(p, cps):
        for cp in cps:
            cp.wait_recv()
        for j in range(2):
            parts = [agp[p, a, i * 2 + j] for a in range(8) for i in range(4)]
            whole = jnp.concatenate(parts, axis=0).astype(F32)
            lg_ref[pl.ds(p * HB, HB), pl.ds(j * E, E)] = whole.T

    out = pair(0)
    acc[0] = out[:, :256]
    acc[1] = out[:, 256:]
    to_across1.wait_recv()
    for cp in to_ring:
        go(cp)
    for cp in to_partner:
        cp.wait_recv()
    out = pair(2)
    d0 = die_send(0, out[:, :256])
    d1 = die_send(1, out[:, 256:])
    lax.fori_loop(0, 4, state_grad(True), 0)
    y0 = y_send(0, d0, acc[0])
    lax.fori_loop(4, 8, state_grad(True), 0)
    to_across0.wait_recv()
    go(to_fwd[0])
    for cp in to_ring:
        cp.wait_recv()
    go(to_fwd[1])
    y1 = y_send(1, d1, acc[1])
    to_fwd[0].wait_recv()
    out = pair(4)
    d2 = die_send(2, out[:, :256])
    acc[2] = out[:, 256:]
    to_fwd[1].wait_recv()
    y2 = y_send(2, d2, acc[2])
    out = pair(6)
    d3 = die_send(3, out[:, :256])
    acc[3] = out[:, 256:]
    xa0 = x_send_home(0, y0)
    y3 = y_send(3, d3, acc[3])
    xa1 = x_send_home(1, y1)
    xb0 = x_send_away(0, y2)
    lax.fori_loop(0, 6, state_grad(False), 0)
    z0 = z_send(0, [xa0] + xb0)
    xb1 = x_send_away(1, y3)
    lax.fori_loop(6, 8, state_grad(False), 0)
    az0 = az_send(0, z0)
    z1 = z_send(1, [xa1] + xb1)
    ap0 = ap_send(0, az0)
    az1 = az_send(1, z1)
    ap1 = ap_send(1, az1)
    finish(0, ap0)
    finish(1, ap1)
    for cp in pending:
        cp.wait_send()


def writer(a, b, c, oa, ob, oc, sem):
    copies = [pltpu.make_async_copy(src, dst, sem.at[i]) for i, (src, dst) in enumerate(((b, ob), (c, oc), (a, oa)))]
    for cp in copies:
        cp.start()
    for cp in copies:
        cp.wait()


def per_device(encoded, queries, classifiers, lengths, beam, logit_grad):
    hbm = pl.BlockSpec(memory_space=pltpu.HBM)
    vm = pl.BlockSpec(memory_space=pltpu.VMEM)
    dma = pltpu.SemaphoreType.DMA
    logits, eg, lg = pl.pallas_call(
        body,
        out_shape=(
            jax.ShapeDtypeStruct((DOCS, 1024), F32),
            jax.ShapeDtypeStruct((T, E), BF16),
            jax.ShapeDtypeStruct((256, 1024), F32),
        ),
        in_specs=[hbm] * 6,
        out_specs=(vm, vm, vm),
        scratch_shapes=[
            pltpu.VMEM((T, E), BF16),
            pltpu.VMEM((E, T), BF16),
            pltpu.VMEM((8, 256, E), BF16),
            pltpu.VMEM((T, 2048), BF16),
            pltpu.VMEM((T, 512), F32),
            pltpu.SMEM((DOCS,), jnp.int32),
            pltpu.VMEM((DOCS, 1024), jnp.int32),
            pltpu.VMEM((DOCS, 1024), F32),
            pltpu.VMEM((DOCS, 1024), F32),
            pltpu.VMEM((4, E, 256), F32),
            pltpu.VMEM((T, E), F32),
            pltpu.VMEM((4, E, 256), BF16),
            pltpu.VMEM((4, E, 256), BF16),
            pltpu.VMEM((4, 4, 128, 256), BF16),
            pltpu.VMEM((4, 3, 128, 256), BF16),
            pltpu.VMEM((4, 4, 128, 256), F32),
            pltpu.VMEM((4, 2, 64, 256), BF16),
            pltpu.VMEM((2, 3, 64, 256), BF16),
            pltpu.VMEM((2, 2, 64, 256), F32),
            pltpu.VMEM((2, 8, 16, 128), BF16),
            pltpu.VMEM((2, 7, 16, 128), BF16),
            pltpu.VMEM((2, 8, 16, 128), F32),
            pltpu.VMEM((2, 8, 8, 16, 128), BF16),
            dma((11,)),
            dma((9,)), dma((9,)),
            dma((4,)), dma((4,)),
            dma((4, 3)), dma((4, 3)),
            dma((2, 3)), dma((2, 3)),
            dma((2, 7)), dma((2, 7)),
            dma((2, 7)), dma((2, 7)),
            dma((2, 7)), dma((2, 7)),
        ],
        compiler_params=pltpu.CompilerParams(
            collective_id=0, has_side_effects=True, vmem_limit_bytes=46 * 1024 * 1024
        ),
        name="attn",
    )(*[
        pltpu.with_memory_space_constraint(v, pltpu.HBM)
        for v in (encoded.reshape(T, E), queries, classifiers, lengths, beam, logit_grad)
    ])
    logits, eg, lg = pl.pallas_call(
        writer,
        out_shape=(
            jax.ShapeDtypeStruct((DOCS, 1024), F32),
            jax.ShapeDtypeStruct((T, E), BF16),
            jax.ShapeDtypeStruct((256, 1024), F32),
        ),
        in_specs=[pl.BlockSpec(memory_space=pl.ANY)] * 3,
        out_specs=(hbm, hbm, hbm),
        scratch_shapes=[dma((3,))],
        compiler_params=pltpu.CompilerParams(vmem_limit_bytes=4 * 1024 * 1024),
        name="writer",
    )(logits, eg, lg)
    return logits, eg.reshape(DOCS, L, E), lg


def solution(mesh):
    in_specs = (
        P(("rep", "blk"), None, None),
        P("blk", None),
        P("blk", None),
        P(("rep", "blk")),
        P(("rep", "blk"), None),
        P(("rep", "blk"), None),
    )
    out_specs = (P(("rep", "blk"), None), P(("rep", "blk"), None, None), P("blk", None))
    return jax.shard_map(
        per_device, mesh=mesh, in_specs=in_specs, out_specs=out_specs, check_vma=False
    )
```

```python
import jax
import jax.numpy as jnp
from jax import lax
from jax.experimental import pallas as pl
from jax.experimental.pallas import tpu as pltpu
from jax.sharding import PartitionSpec as P

MESH = pl.DeviceIdType.MESH
F32 = jnp.float32
BF16 = jnp.bfloat16
E = 512
L = 512
DOCS = 4
T = DOCS * L
HB = 128
NEG = -1e30


def body(
    enc_hbm, q_hbm, c_hbm, len_hbm, beam_hbm, grad_hbm,
    logit_ref, eg_ref, lg_ref,
    S, ST, W, GA, SP, len_ref, beam_ref, grad_ref, G, acc, eacc,
    dsend, drecv, ysend, yrecv, yown, xsend, xrecv, xown, zsend, zrecv, zown, agp,
    lsem, gs, gr, ds, dr, ys, yr, xs, xr, zs, zr, as_, ar, ps, pr,
):
    rep = lax.axis_index("rep")
    blk = lax.axis_index("blk")
    x_lo = rep // 32
    z = (rep // 4) % 8
    y = rep % 4
    x_hi = blk // 2
    core = blk % 2

    def dev(xl, zz, yy, xh, cc):
        return ((xl * 8 + zz) * 4 + yy, xh * 2 + cc)

    partner = dev(x_lo, z, y, x_hi, 1 - core)
    across = dev(1 - x_lo, z, y, 1 - x_hi, core)
    across2 = dev(x_lo, z, y, 1 - x_hi, core)
    xpair = dev(1 - x_lo, z, y, x_hi, core)
    place = y * 2 + x_lo

    def ynb(k):
        return dev(x_lo, z, (y + k) % 4, x_hi, core)

    def znb(k):
        return dev(x_lo, (z + k) % 8, y, x_hi, core)

    def pnb(k):
        pp = (place + k) % 8
        return dev(pp % 2, z, pp // 2, x_hi, core)

    def local(src, dst, i):
        cp = pltpu.make_async_copy(src, dst, lsem.at[i])
        cp.start()
        return cp

    def remote(src, dst, ssem, rsem, to):
        return pltpu.make_async_remote_copy(
            src_ref=src, dst_ref=dst, send_sem=ssem, recv_sem=rsem,
            device_id=to, device_id_type=MESH,
        )

    pending = []

    def go(cp):
        cp.start()
        pending.append(cp)
        return cp

    weights = []
    for p in range(2):
        weights.append(local(q_hbm.at[pl.ds(p * HB, HB)], W.at[p, pl.ds(0, HB)], 2 * p))
        weights.append(local(c_hbm.at[pl.ds(p * HB, HB)], W.at[p, pl.ds(HB, HB)], 2 * p + 1))
    states = [local(enc_hbm.at[pl.ds(d * L, L)], S.at[pl.ds(d * L, L)], 4 + d) for d in range(DOCS)]

    small = [local(beam_hbm, beam_ref, 8), local(grad_hbm, grad_ref, 9), local(len_hbm, len_ref, 10)]

    barrier = pltpu.get_barrier_semaphore()
    greet = [partner, across, across2] + [znb(k) for k in range(1, 8)] + [pnb(k) for k in range(1, 8)]
    for to in greet:
        pl.semaphore_signal(barrier, inc=1, device_id=to, device_id_type=MESH)
    for cp in weights:
        cp.wait()
    pl.semaphore_wait(barrier, len(greet))

    to_partner = [go(remote(W.at[p], W.at[2 + p], gs.at[p], gr.at[p], partner)) for p in range(2)]
    quarter = pl.ds(pl.multiple_of(y * 48, 16), 48)
    to_across1 = go(remote(W.at[1, quarter], W.at[7, quarter], gs.at[2], gr.at[2], across))
    to_across0 = go(remote(W.at[0], W.at[5], gs.at[3], gr.at[3], across))
    rest = pl.ds(192, 64)
    to_across2 = go(remote(W.at[1, rest], W.at[7, rest], gs.at[9], gr.at[9], across))
    to_ring = [
        remote(W.at[7, quarter], W.at[7, quarter], gs.at[5 + k], gr.at[5 + k], ynb(k)) for k in (2, 1, 3)
    ]
    to_fwd = [remote(W.at[5 + 2 * p], W.at[4 + 2 * p], gs.at[4 + p], gr.at[4 + p], partner) for p in range(2)]

    for cp in small:
        cp.wait()
    G[...] = grad_ref[...] * beam_ref[...].astype(F32)
    for d in range(DOCS):
        states[d].wait()
        ST[:, pl.ds(d * L, L)] = S[pl.ds(d * L, L), :].T

    own0 = blk * 256
    par0 = (x_hi * 2 + 1 - core) * 256
    far_own0 = ((1 - x_hi) * 2 + core) * 256
    far_par0 = ((1 - x_hi) * 2 + 1 - core) * 256
    starts = [own0, own0 + HB, par0, par0 + HB, far_par0, far_own0, far_par0 + HB, far_own0 + HB]

    row = lax.broadcasted_iota(jnp.int32, (L, HB), 0)

    def pair(k, last=False):
        ats = [pl.ds(pl.multiple_of(starts[k + i], HB), HB) for i in range(2)]
        w = W[pl.ds(k, 2)].reshape(512, E)
        g = [[G[pl.ds(d, 1), at] for at in ats] for d in range(DOCS)]

        def scores(d):
            SP[pl.ds(d * L, L), :] = lax.dot_general(
                S[pl.ds(d * L, L), :], w, (((1,), (1,)), ((), ())), preferred_element_type=F32
            )

        def soft(d):
            rows = pl.ds(d * L, L)
            valid = row < len_ref[d]
            for i in range(2):
                sc = jnp.where(valid, SP[rows, pl.ds(i * 256, HB)], NEG)
                pr_ = SP[rows, pl.ds(i * 256 + HB, HB)]
                ex = jnp.exp(sc - jnp.max(sc, axis=0, keepdims=True))
                inv = 1.0 / jnp.sum(ex, axis=0, keepdims=True)
                lg = jnp.sum(ex * pr_, axis=0, keepdims=True) * inv
                logit_ref[pl.ds(d, 1), ats[i]] = lg
                ag = ex * (inv * g[d][i])
                GA[rows, pl.ds((k + i) * 256 + HB, HB)] = ag.astype(BF16)
                GA[rows, pl.ds((k + i) * 256, HB)] = (ag * (pr_ - lg)).astype(BF16)

        def lab(d):
            rows = pl.ds(d * L, 2 * L)
            return jnp.dot(ST[:, rows], GA[rows, pl.ds(k * 256, 512)], preferred_element_type=F32)

        scores(0)
        scores(1)
        soft(0)
        scores(2)
        soft(1)
        if last:
            scores(3)
            soft(2)
            soft(3)
            return None
        out = lab(0)
        scores(3)
        soft(2)
        soft(3)
        return out + lab(2)

    def state_grad(first):
        def tile(i, carry):
            rows = pl.ds(pl.multiple_of(i * 256, 256), 256)
            if first:
                eacc[rows, :] = jnp.dot(
                    GA[rows, pl.ds(0, 1024)], W[pl.ds(0, 4)].reshape(1024, E), preferred_element_type=F32
                )
            else:
                eg_ref[rows, :] = (
                    eacc[rows, :]
                    + jnp.dot(
                        GA[rows, pl.ds(1024, 1024)], W[pl.ds(4, 4)].reshape(1024, E), preferred_element_type=F32
                    )
                ).astype(BF16)
            return carry

        return tile

    def die_send(j, value):
        dsend[j] = value.astype(BF16)
        return go(remote(dsend.at[j], drecv.at[j], ds.at[j], dr.at[j], partner))

    def y_send(j, dcp, own):
        dcp.wait_recv()
        total = own + drecv[j].astype(F32)
        yown[j] = total.reshape(4, 128, 256)
        ysend[j] = total.astype(BF16).reshape(4, 128, 256)
        return [
            go(remote(ysend.at[j, (y + k) % 4], yrecv.at[j, k - 1], ys.at[j, k - 1], yr.at[j, k - 1], ynb(k)))
            for k in range(1, 4)
        ]

    def last_sends():
        places = {k: pl.ds(pl.multiple_of(((y + k) % 4) * 128, 128), 128) for k in range(4)}
        die, cps = {}, []
        for ks in ((2, 1), (3, 0)):
            lhs = jnp.concatenate([ST[places[k], :] for k in ks], axis=0)
            out = jnp.dot(lhs, GA[:, pl.ds(6 * 256, 512)], preferred_element_type=F32)
            for n, k in enumerate(ks):
                dsend[3, places[k], :] = out[n * 128 : (n + 1) * 128, :256].astype(BF16)
                acc[3, places[k], :] = out[n * 128 : (n + 1) * 128, 256:]
                die[k] = go(remote(dsend.at[3, places[k]], drecv.at[3, places[k]], ds.at[3 + k], dr.at[3 + k], partner))
        for k in (2, 1, 3, 0):
            yp = (y + k) % 4
            die[k].wait_recv()
            total = acc[3, places[k], :] + drecv[3, places[k], :].astype(F32)
            if k:
                ysend[3, yp] = total.astype(BF16)
                cps.append(go(remote(ysend.at[3, yp], yrecv.at[3, k - 1], ys.at[3, k - 1], yr.at[3, k - 1], ynb(k))))
            else:
                yown[3, yp] = total
        return cps

    def y_sum(j, cps):
        for cp in cps:
            cp.wait_recv()
        total = yown[j, y]
        for k in range(3):
            total = total + yrecv[j, k].astype(F32)
        return total

    def x_send_home(p, cps):
        total = y_sum(p, cps).reshape(2, 64, 256)
        xown[p] = total
        xsend[p] = total.astype(BF16)
        return go(remote(xsend.at[p, 1 - x_lo], xrecv.at[p, 0], xs.at[p, 0], xr.at[p, 0], xpair))

    def x_send_away(p, cps):
        total = y_sum(2 + p, cps).reshape(2, 64, 256)
        xsend[2 + p] = total.astype(BF16)
        return [
            go(remote(xsend.at[2 + p, x_lo], xrecv.at[p, 1], xs.at[p, 1], xr.at[p, 1], across2)),
            go(remote(xsend.at[2 + p, 1 - x_lo], xrecv.at[p, 2], xs.at[p, 2], xr.at[p, 2], across)),
        ]

    def z_send(p, cps):
        for cp in cps:
            cp.wait_recv()
        total = xown[p, x_lo]
        for k in range(3):
            total = total + xrecv[p, k].astype(F32)
        for i in range(4):
            for j in range(2):
                piece = total[i * 16 : (i + 1) * 16, j * 128 : (j + 1) * 128]
                zown[p, i * 2 + j] = piece
                zsend[p, i * 2 + j] = piece.astype(BF16)
        return [
            go(remote(zsend.at[p, (z + k) % 8], zrecv.at[p, k - 1], zs.at[p, k - 1], zr.at[p, k - 1], znb(k)))
            for k in range(1, 8)
        ]

    def az_send(p, cps):
        for cp in cps:
            cp.wait_recv()
        total = zown[p, z]
        for k in range(7):
            total = total + zrecv[p, k].astype(F32)
        agp[p, place, z] = total.astype(BF16)
        return [
            go(remote(agp.at[p, place, z], agp.at[p, place, z], as_.at[p, k - 1], ar.at[p, k - 1], znb(k)))
            for k in range(1, 8)
        ]

    def ap_send(p, cps):
        for cp in cps:
            cp.wait_recv()
        return [
            go(remote(agp.at[p, place], agp.at[p, place], ps.at[p, k - 1], pr.at[p, k - 1], pnb(k)))
            for k in range(1, 8)
        ]

    def finish(p, cps):
        for cp in cps:
            cp.wait_recv()
        for j in range(2):
            parts = [agp[p, a, i * 2 + j] for a in range(8) for i in range(4)]
            whole = jnp.concatenate(parts, axis=0).astype(F32)
            lg_ref[pl.ds(p * HB, HB), pl.ds(j * E, E)] = whole.T

    out = pair(0)
    acc[0] = out[:, :256]
    acc[1] = out[:, 256:]
    to_across1.wait_recv()
    for cp in to_ring:
        go(cp)
    for cp in to_partner:
        cp.wait_recv()
    out = pair(2)
    d0 = die_send(0, out[:, :256])
    d1 = die_send(1, out[:, 256:])
    lax.fori_loop(0, 4, state_grad(True), 0)
    y0 = y_send(0, d0, acc[0])
    y1 = y_send(1, d1, acc[1])
    to_across0.wait_recv()
    go(to_fwd[0])
    for cp in to_ring + [to_across2]:
        cp.wait_recv()
    go(to_fwd[1])
    to_fwd[0].wait_recv()
    out = pair(4)
    d2 = die_send(2, out[:, :256])
    acc[2] = out[:, 256:]
    lax.fori_loop(4, 8, state_grad(True), 0)
    to_fwd[1].wait_recv()
    y2 = y_send(2, d2, acc[2])
    pair(6, True)
    y3 = last_sends()
    xa0 = x_send_home(0, y0)
    xa1 = x_send_home(1, y1)
    xb0 = x_send_away(0, y2)
    lax.fori_loop(0, 6, state_grad(False), 0)
    z0 = z_send(0, [xa0] + xb0)
    xb1 = x_send_away(1, y3)
    lax.fori_loop(6, 8, state_grad(False), 0)
    az0 = az_send(0, z0)
    z1 = z_send(1, [xa1] + xb1)
    ap0 = ap_send(0, az0)
    az1 = az_send(1, z1)
    ap1 = ap_send(1, az1)
    finish(0, ap0)
    finish(1, ap1)
    for cp in pending:
        cp.wait_send()


def writer(a, b, c, oa, ob, oc, sem):
    copies = [pltpu.make_async_copy(src, dst, sem.at[i]) for i, (src, dst) in enumerate(((b, ob), (c, oc), (a, oa)))]
    for cp in copies:
        cp.start()
    for cp in copies:
        cp.wait()


def per_device(encoded, queries, classifiers, lengths, beam, logit_grad):
    hbm = pl.BlockSpec(memory_space=pltpu.HBM)
    vm = pl.BlockSpec(memory_space=pltpu.VMEM)
    dma = pltpu.SemaphoreType.DMA
    logits, eg, lg = pl.pallas_call(
        body,
        out_shape=(
            jax.ShapeDtypeStruct((DOCS, 1024), F32),
            jax.ShapeDtypeStruct((T, E), BF16),
            jax.ShapeDtypeStruct((256, 1024), F32),
        ),
        in_specs=[hbm] * 6,
        out_specs=(vm, vm, vm),
        scratch_shapes=[
            pltpu.VMEM((T, E), BF16),
            pltpu.VMEM((E, T), BF16),
            pltpu.VMEM((8, 256, E), BF16),
            pltpu.VMEM((T, 2048), BF16),
            pltpu.VMEM((T, 512), F32),
            pltpu.SMEM((DOCS,), jnp.int32),
            pltpu.VMEM((DOCS, 1024), jnp.int32),
            pltpu.VMEM((DOCS, 1024), F32),
            pltpu.VMEM((DOCS, 1024), F32),
            pltpu.VMEM((4, E, 256), F32),
            pltpu.VMEM((T, E), F32),
            pltpu.VMEM((4, E, 256), BF16),
            pltpu.VMEM((4, E, 256), BF16),
            pltpu.VMEM((4, 4, 128, 256), BF16),
            pltpu.VMEM((4, 3, 128, 256), BF16),
            pltpu.VMEM((4, 4, 128, 256), F32),
            pltpu.VMEM((4, 2, 64, 256), BF16),
            pltpu.VMEM((2, 3, 64, 256), BF16),
            pltpu.VMEM((2, 2, 64, 256), F32),
            pltpu.VMEM((2, 8, 16, 128), BF16),
            pltpu.VMEM((2, 7, 16, 128), BF16),
            pltpu.VMEM((2, 8, 16, 128), F32),
            pltpu.VMEM((2, 8, 8, 16, 128), BF16),
            dma((11,)),
            dma((10,)), dma((10,)),
            dma((7,)), dma((7,)),
            dma((4, 3)), dma((4, 3)),
            dma((2, 3)), dma((2, 3)),
            dma((2, 7)), dma((2, 7)),
            dma((2, 7)), dma((2, 7)),
            dma((2, 7)), dma((2, 7)),
        ],
        compiler_params=pltpu.CompilerParams(
            collective_id=0, has_side_effects=True, vmem_limit_bytes=46 * 1024 * 1024
        ),
        name="attn",
    )(*[
        pltpu.with_memory_space_constraint(v, pltpu.HBM)
        for v in (encoded.reshape(T, E), queries, classifiers, lengths, beam, logit_grad)
    ])
    logits, eg, lg = pl.pallas_call(
        writer,
        out_shape=(
            jax.ShapeDtypeStruct((DOCS, 1024), F32),
            jax.ShapeDtypeStruct((T, E), BF16),
            jax.ShapeDtypeStruct((256, 1024), F32),
        ),
        in_specs=[pl.BlockSpec(memory_space=pl.ANY)] * 3,
        out_specs=(hbm, hbm, hbm),
        scratch_shapes=[dma((3,))],
        compiler_params=pltpu.CompilerParams(vmem_limit_bytes=4 * 1024 * 1024),
        name="writer",
    )(logits, eg, lg)
    return logits, eg.reshape(DOCS, L, E), lg


def solution(mesh):
    in_specs = (
        P(("rep", "blk"), None, None),
        P("blk", None),
        P("blk", None),
        P(("rep", "blk")),
        P(("rep", "blk"), None),
        P(("rep", "blk"), None),
    )
    out_specs = (P(("rep", "blk"), None), P(("rep", "blk"), None, None), P("blk", None))
    return jax.shard_map(
        per_device, mesh=mesh, in_specs=in_specs, out_specs=out_specs, check_vma=False
    )
```
